32 devices in a mesh: users: 16 (over z, y, x), rep: 2 (over core).
Axes of the slice: x: 2, y: 2, z: 4, core: 2. Of those that a mesh axis runs over, the one named last changes fastest.
Arguments:
- user_factors: float32 [16384, 256], P('users'), may hold values from -1.5 to 1.5
- user_accum: float32 [16384, 256], P('users'), may hold values from 0.5 to 8
- item_factors: float32 [4096, 256], P('users'), may hold values from -1.5 to 1.5
- item_accum: float32 [4096, 256], P('users'), may hold values from 0.5 to 8
- tile_counts: bfloat16 [16, 2, 128, 128, 128], P('users', 'rep'), may hold values from 0 to 20, as said below
- tile_user: int32 [16, 2, 128], P('users', 'rep'), may hold values from 0 to 7
- tile_item: int32 [16, 2, 128], P('users', 'rep'), may hold values from 0 to 31, as said below
- send_list: int32 [16, 2, 16], P('users', 'rep'), may hold values from 0 to 2, as said below
Outputs:
- new_users: float32 [16384, 256], P('users')
- new_user_accum: float32 [16384, 256], P('users')
- new_items: float32 [4096, 256], P('users')
- new_item_accum: float32 [4096, 256], P('users')
The draws below stay inside these ranges and needn't reach their ends.
Inputs may be any that keep to these rules, and one draw needn't show every extreme that they name: `tile_counts`: zero means no interaction. `tile_item`: panel b belongs to owner b // 2. Device (q, r) uses at most one panel of each owner o, namely o * 2 + send_list[o, r, q], and only where send_list[o, r, q] < 2. `send_list`: the value 2 means that requester q uses no panel of owner o.
All inputs are finite; a program needn't handle non-finite values.
Results may differ from the reference program's by a relative error of at most 0.0026.
Values may be sent and summed in bfloat16 or wider, within the bound.
No kernel may reach another device: no remote copies, remote signals or barrier semaphores. Data moves between devices by JAX's collectives and lax.ppermute only.
A program may use at most 128 MiB of HBM per device.

```python
import math
import jax
import jax.numpy as jnp
from jax import lax

R = 256
TILE = 128
UB = 8
TILES = 128
IPD = 2
USERS = 16384
ITEMS = 4096
N_USERS = 16
N_REP = 2


def request_table(key):
    base_key = jax.random.fold_in(key, 101)
    kept_slot = jax.random.randint(jax.random.fold_in(base_key, 1), (N_USERS, N_REP, N_USERS), 0, 10) >= 3
    own_slot = jnp.arange(N_USERS)[:, None, None] == jnp.arange(N_USERS)[None, None, :]
    kept_slot = kept_slot | own_slot
    picked = jax.random.randint(jax.random.fold_in(base_key, 2), (N_USERS, N_REP, N_USERS), 0, IPD)
    return jnp.where(kept_slot, picked, IPD).astype(jnp.int32)


def draw_tile_item(key, part):
    table = request_table(key)
    scores = jax.random.randint(jax.random.fold_in(key, 202), (N_USERS, N_REP, TILES, N_USERS), 0, 2 ** 20)
    scores = scores + jnp.where(table < IPD, 2 ** 21, 0)[:, :, None, :]
    owner_pick = jnp.argmax(scores, axis=-1).astype(jnp.int32)
    spread = jnp.broadcast_to(table[:, :, None, :], scores.shape)
    panel_pick = jnp.take_along_axis(spread, owner_pick[..., None], axis=-1)[..., 0]
    return (owner_pick * IPD + panel_pick).astype(jnp.int32)


def draw_send_list(key, part):
    return jnp.transpose(request_table(key), (2, 1, 0)).astype(jnp.int32)


def draw_tile_counts(key, part):
    shape = (N_USERS, N_REP, TILES, TILE, TILE)
    coin = jax.random.uniform(jax.random.fold_in(key, 303), shape, jnp.float32)
    level = jax.random.uniform(jax.random.fold_in(key, 304), shape, jnp.float32)
    nonzero = coin < 0.35
    amounts = jnp.exp(level * jnp.log(20.0))
    return jnp.where(nonzero, amounts, 0.0).astype(jnp.bfloat16)


def plant(entries, stream_key, low, largest):
    index_at = [jax.random.randint(jax.random.fold_in(stream_key, axis), (), 0, length) for axis, length in enumerate(entries.shape)]
    main_axis = entries.shape.index(max(entries.shape))
    beside = index_at[:main_axis] + [(index_at[main_axis] + 1) % entries.shape[main_axis]] + index_at[main_axis + 1:]
    return entries.at[tuple(index_at)].set(low).at[tuple(beside)].set(largest)


def levels(key, dims, split, smallest, top_value):
    gain, own = 1.0, jax.random.fold_in(key, 6)
    for position, shards_of in split:
        heights = jnp.exp(jax.random.uniform(jax.random.fold_in(own, position), (shards_of,), jnp.float32, smallest / len(split), top_value / len(split)))
        gain = gain * jnp.repeat(heights, dims[position] // shards_of).reshape([-1 if axis == position else 1 for axis in range(len(dims))])
    return gain


def gaussian(rng, shape, scale, reach, split=(), kind=jnp.bfloat16):
    array = scale * jax.random.normal(rng, shape, jnp.float32)
    if split:
        array = array * levels(rng, shape, split, -0.22, 0.18)
    return jnp.clip(array, -reach, reach).astype(kind)


def setup_inputs(seed: int = 0) -> dict:
    keys = jax.random.split(jax.random.key(seed), 9)
    user_factors = gaussian(keys[0], (USERS, R), 0.25, 1.5, ((0, 16),), jnp.float32)
    user_accum = jnp.clip(jnp.exp(math.log(8.0) - 2.7725887 * jax.random.uniform(keys[1], (USERS, R), jnp.float32) ** levels(keys[1], (USERS, R), ((0, 16),), -0.2, 0.2)), 0.5, 8.0)
    item_factors = gaussian(keys[2], (ITEMS, R), 0.25, 1.5, ((0, 16),), jnp.float32)
    item_accum = jnp.clip(jnp.exp(math.log(8.0) - 2.7725887 * jax.random.uniform(keys[3], (ITEMS, R), jnp.float32) ** levels(keys[3], (ITEMS, R), ((0, 16),), -0.2, 0.2)), 0.5, 8.0)
    tile_counts = draw_tile_counts(jax.random.fold_in(keys[8], 71), 0)
    tile_user = plant(jax.random.randint(keys[5], (N_USERS, N_REP, TILES), 0, UB), jax.random.fold_in(keys[5], 1), 0, UB - 1).astype(jnp.int32)
    tile_item = draw_tile_item(jax.random.fold_in(keys[8], 71), 0)
    send_list = draw_send_list(jax.random.fold_in(keys[8], 71), 0)
    return {"user_factors": user_factors, "user_accum": user_accum, "item_factors": item_factors, "item_accum": item_accum, "tile_counts": tile_counts, "tile_user": tile_user, "tile_item": tile_item, "send_list": send_list}


CONF_SLOPE = 0.5
ERR_SCALE = 1.0 / 64.0

def tile_terms(user_strip, panels, counts, users_idx, fetch_index, slot_index, slot_count):
    tile_count = counts.shape[0]
    group_size = math.gcd(tile_count, 32)
    group_count = tile_count // group_size
    side = counts.shape[-1]
    width = panels.shape[-1]

    def tile_step(totals, inputs):
        user_total, slot_total = totals
        block_counts, block_user, block_fetch, block_slot = inputs
        user_rows = user_strip[block_user].astype(jnp.float32)
        item_rows = panels[block_fetch].astype(jnp.float32)
        predicted = jnp.einsum('gur,gir->gui', user_rows, item_rows)
        amount = block_counts.astype(jnp.float32)
        confidence = 1.0 + CONF_SLOPE * amount
        preference = jnp.where(amount > 0, 1.0, 0.0).astype(jnp.float32)
        weighted_err = lax.optimization_barrier((confidence * (predicted - preference) * ERR_SCALE).astype(jnp.bfloat16))
        weighted_err = weighted_err.astype(jnp.float32)
        user_part = jnp.einsum('gui,gir->gur', weighted_err, item_rows)
        item_part = jnp.einsum('gui,gur->gir', weighted_err, user_rows)
        user_total = user_total.at[block_user].add(user_part)
        slot_total = slot_total.at[block_slot].add(item_part)
        return ((user_total, slot_total), None)
    start = (jnp.zeros((user_strip.shape[0], side, width), jnp.float32), jnp.zeros((slot_count, side, width), jnp.float32))
    inputs = (counts.reshape(group_count, group_size, side, side), users_idx.reshape(group_count, group_size).astype(jnp.int32), fetch_index.reshape(group_count, group_size).astype(jnp.int32), slot_index.reshape(group_count, group_size).astype(jnp.int32))
    (user_total, slot_total), _ = lax.scan(tile_step, start, inputs)
    return (user_total, slot_total)

def reference(user_factors, user_accum, item_factors, item_accum, tile_counts, tile_user, tile_item, send_list):
    strips = user_factors.astype(jnp.bfloat16).reshape(N_USERS, UB, TILE, R)
    panels = item_factors.astype(jnp.bfloat16).reshape(N_USERS * IPD, TILE, R)

    def per_strip(item_grad, inputs):
        user_strip, counts, users_idx, items_idx, strip_index = inputs
        user_grad = jnp.zeros((UB, TILE, R), jnp.float32)
        for rep_index in range(N_REP):
            user_part, slot_part = tile_terms(user_strip, panels, counts[rep_index], users_idx[rep_index], items_idx[rep_index], items_idx[rep_index] // IPD, N_USERS)
            user_grad = user_grad + user_part
            rounded = lax.optimization_barrier(slot_part.astype(jnp.bfloat16)).astype(jnp.float32)
            panel_of = send_list[:, rep_index, strip_index]
            target = jnp.arange(N_USERS, dtype=jnp.int32) * IPD + jnp.minimum(panel_of, IPD - 1).astype(jnp.int32)
            item_grad = item_grad.at[target].add(rounded)
        return (item_grad, user_grad)
    item_grad, user_grads = lax.scan(per_strip, jnp.zeros((N_USERS * IPD, TILE, R), jnp.float32), (strips, tile_counts, tile_user, tile_item, jnp.arange(N_USERS, dtype=jnp.int32)))
    user_grad = user_grads.reshape(USERS, R)
    item_grad = item_grad.reshape(ITEMS, R)
    new_user_accum = user_accum + user_grad * user_grad
    new_users = user_factors - user_grad / jnp.sqrt(new_user_accum)
    new_item_accum = item_accum + item_grad * item_grad
    new_items = item_factors - item_grad / jnp.sqrt(new_item_accum)
    return (new_users, new_user_accum, new_items, new_item_accum)
```

```python
import functools
import math

import jax
import jax.numpy as jnp
from jax import lax
from jax.experimental import pallas as pl
from jax.experimental.pallas import tpu as pltpu
from jax.sharding import PartitionSpec as P


CONF_SLOPE = 0.5
ERR_SCALE = 1.0 / 64.0
DENSE_LIMIT = 32 * 1024 * 1024
TABLE_VMEM = 24 * 1024 * 1024
GRAD_VMEM = 32 * 1024 * 1024
TWO_PART = True
GROUP = 4


def tile_terms(user_strip, panels, counts, users_idx, fetch_index, slot_index, slot_count):
    tile_count = counts.shape[0]
    group_size = math.gcd(tile_count, 32)
    group_count = tile_count // group_size
    side = counts.shape[-1]
    width = panels.shape[-1]

    def tile_step(totals, inputs):
        user_total, slot_total = totals
        block_counts, block_user, block_fetch, block_slot = inputs
        user_rows = user_strip[block_user]
        item_rows = panels[block_fetch]
        predicted = jnp.einsum(
            "gur,gir->gui", user_rows, item_rows, preferred_element_type=jnp.float32
        )
        amount = block_counts.astype(jnp.float32)
        confidence = 1.0 + CONF_SLOPE * amount
        preference = jnp.where(amount > 0, 1.0, 0.0).astype(jnp.float32)
        weighted_err = (confidence * (predicted - preference) * ERR_SCALE).astype(jnp.bfloat16)
        user_part = jnp.einsum(
            "gui,gir->gur", weighted_err, item_rows, preferred_element_type=jnp.float32
        )
        item_part = jnp.einsum(
            "gui,gur->gir", weighted_err, user_rows, preferred_element_type=jnp.float32
        )
        user_total = user_total.at[block_user].add(user_part)
        slot_total = slot_total.at[block_slot].add(item_part)
        return ((user_total, slot_total), None)

    start = (
        jnp.zeros((user_strip.shape[0], side, width), jnp.float32),
        jnp.zeros((slot_count, side, width), jnp.float32),
    )
    inputs = (
        counts.reshape(group_count, group_size, side, side),
        users_idx.reshape(group_count, group_size),
        fetch_index.reshape(group_count, group_size),
        slot_index.reshape(group_count, group_size),
    )
    (user_total, slot_total), _ = lax.scan(tile_step, start, inputs)
    return (user_total, slot_total)


def adagrad(factors, accum, grad):
    new_accum = accum + grad * grad
    return (factors - grad / jnp.sqrt(new_accum), new_accum)


def local_tiles(
    user_factors, user_accum, item_factors, item_accum, tile_counts, tile_user, tile_item, send_list
):
    tile_size = tile_counts.shape[-1]
    feat_width = user_factors.shape[1]
    user_strip = user_factors.astype(jnp.bfloat16).reshape(-1, tile_size, feat_width)
    owned_panels = item_factors.astype(jnp.bfloat16).reshape(-1, tile_size, feat_width)
    panels_own = owned_panels.shape[0]
    peer_count = lax.axis_size("users")
    counts = tile_counts[0, 0]
    users_idx = tile_user[0, 0]
    items_idx = tile_item[0, 0]
    send_row = send_list[0, 0]
    slot_index = items_idx // panels_own
    outgoing = owned_panels[jnp.minimum(send_row, panels_own - 1)]
    panels = lax.all_to_all(outgoing, "users", split_axis=0, concat_axis=0, tiled=True)
    user_part, slot_part = tile_terms(
        user_strip, panels, counts, users_idx, slot_index, slot_index, peer_count
    )
    returned = lax.all_to_all(
        slot_part.astype(jnp.bfloat16), "users", split_axis=0, concat_axis=0, tiled=True
    )
    selector = (send_row[None, :] == jnp.arange(panels_own, dtype=jnp.int32)[:, None]).astype(
        jnp.bfloat16
    )
    item_part = jnp.einsum("kq,qir->kir", selector, returned, preferred_element_type=jnp.float32)
    item_part = item_part.reshape(-1, feat_width)
    user_grad = lax.psum(user_part.reshape(-1, feat_width), "rep")
    new_users, new_user_accum = adagrad(user_factors, user_accum, user_grad)
    item_grad = lax.psum(item_part, "rep")
    new_items, new_item_accum = adagrad(item_factors, item_accum, item_grad)
    return (new_users, new_user_accum, new_items, new_item_accum)


def combine_kernel(own, par, out, sems):
    tiles = own.shape[0]
    first = pltpu.make_async_copy(own, out.at[pl.ds(0, tiles)], sems.at[0])
    second = pltpu.make_async_copy(par, out.at[pl.ds(tiles, tiles)], sems.at[1])
    first.start()
    second.start()
    first.wait()
    second.wait()


def combine(own, par):
    tiles, side, _ = own.shape
    anywhere = pl.BlockSpec(memory_space=pl.ANY)
    return pl.pallas_call(
        combine_kernel,
        out_shape=jax.ShapeDtypeStruct((2 * tiles, side, side), own.dtype),
        in_specs=[anywhere, anywhere],
        out_specs=anywhere,
        scratch_shapes=[pltpu.SemaphoreType.DMA((2,))],
        compiler_params=pltpu.CompilerParams(vmem_limit_bytes=TABLE_VMEM),
        name="combine",
    )(own, par)


def table_kernel(order, begin, counts, s_ref, n_ref):
    step = pl.program_id(0)
    side = s_ref.shape[-1]
    blocks = s_ref.shape[1] // side

    def block(ub, _):
        pair = step * blocks + ub
        first, end = begin[pair], begin[pair + 1]
        rows = pl.ds(pl.multiple_of(ub * side, side), side)

        def terms(k):
            count = counts[order[k]]
            hit = jnp.where(count > 0, jnp.bfloat16(ERR_SCALE), jnp.bfloat16(0.0))
            return count.astype(jnp.float32) * (CONF_SLOPE * ERR_SCALE), hit

        @pl.when(first == end)
        def _():
            s_ref[0, rows, :] = jnp.zeros((side, side), jnp.float32)
            n_ref[0, rows, :] = jnp.zeros((side, side), jnp.bfloat16)

        @pl.when(first < end)
        def _():
            half, hit = terms(first)
            s_ref[0, rows, :] = half
            n_ref[0, rows, :] = hit

        def more(k, _):
            half, hit = terms(k)
            s_ref[0, rows, :] += half
            n_ref[0, rows, :] += hit
            return 0

        lax.fori_loop(first + 1, end, more, 0)
        return 0

    lax.fori_loop(0, blocks, block, 0)


def block_tables(order, begin, counts, positions, blocks):
    side = counts.shape[-1]
    spec = pl.BlockSpec((1, blocks * side, side), lambda j: (j, 0, 0))
    shape = (positions, blocks * side, side)
    scalars = pl.BlockSpec(memory_space=pltpu.SMEM)
    return pl.pallas_call(
        table_kernel,
        grid=(positions,),
        out_shape=(
            jax.ShapeDtypeStruct(shape, jnp.float32),
            jax.ShapeDtypeStruct(shape, jnp.bfloat16),
        ),
        in_specs=[scalars, scalars, pl.BlockSpec(memory_space=pltpu.VMEM)],
        out_specs=(spec, spec),
        compiler_params=pltpu.CompilerParams(vmem_limit_bytes=TABLE_VMEM),
        name="tables",
    )(order, begin, counts)


def prepare_kernel(f_ref, u_ref, ut_ref):
    rounded = f_ref[...].astype(jnp.bfloat16)
    u_ref[...] = rounded
    ut_ref[...] = f_ref[...].T.astype(jnp.bfloat16)


def prepare_users(factors):
    strip, width = factors.shape
    step = math.gcd(strip, 512)
    return pl.pallas_call(
        prepare_kernel,
        grid=(strip // step,),
        out_shape=(
            jax.ShapeDtypeStruct((strip, width), jnp.bfloat16),
            jax.ShapeDtypeStruct((width, strip), jnp.bfloat16),
        ),
        in_specs=[pl.BlockSpec((step, width), lambda j: (j, 0))],
        out_specs=(
            pl.BlockSpec((step, width), lambda j: (j, 0)),
            pl.BlockSpec((width, step), lambda j: (0, j)),
        ),
        compiler_params=pltpu.CompilerParams(vmem_limit_bytes=GRAD_VMEM),
        name="prepare",
    )(factors)


def grad_kernel(group, first, tiles_in, u_ref, ut_ref, v_ref, s_ref, n_ref, *refs):
    if first:
        g_ref, p_ref = refs
    else:
        gin_ref, g_ref, p_ref = refs
    step = pl.program_id(0)
    side = s_ref.shape[-1]
    users = u_ref.shape[0]
    blocks = users // side

    @pl.when(step == 0)
    def _():
        g_ref[...] = jnp.zeros_like(g_ref) if first else gin_ref[...]

    panel = v_ref[...].reshape(group * side, v_ref.shape[-1])
    predicted = lax.dot_general(
        u_ref[...], panel, (((1,), (1,)), ((), ())), preferred_element_type=jnp.float32
    )

    columns, rests = [], []
    for k in range(group):
        rows, low = [], []
        for ub in range(blocks):
            weight = tiles_in[(step * group + k) * blocks + ub]
            part = slice(ub * side, (ub + 1) * side)
            half = s_ref[k, part, :]
            hits = n_ref[k, part, :].astype(jnp.float32)
            guess = predicted[part, k * side : (k + 1) * side]
            err = (weight + half) * guess - (hits + half)
            rows.append(err.astype(jnp.bfloat16))
            if TWO_PART:
                low.append((err - rows[-1].astype(jnp.float32)).astype(jnp.bfloat16))
        columns.append(jnp.concatenate(rows, axis=0))
        if TWO_PART:
            rests.append(jnp.concatenate(low, axis=0))
    err = jnp.concatenate(columns, axis=1)
    total = jnp.dot(err, panel, preferred_element_type=jnp.float32)
    item = jnp.dot(ut_ref[...], err, preferred_element_type=jnp.float32)
    if TWO_PART:
        rest = jnp.concatenate(rests, axis=1)
        total += jnp.dot(rest, panel, preferred_element_type=jnp.float32)
        item += jnp.dot(ut_ref[...], rest, preferred_element_type=jnp.float32)
    g_ref[...] += total
    for k in range(group):
        p_ref[k] = item[:, k * side : (k + 1) * side].astype(p_ref.dtype)


def gradients(tiles_in, users, users_t, panels, s_tab, n_tab, g_in, out_dtype):
    count, side, width = panels.shape
    strip = users.shape[0]
    group = math.gcd(count, GROUP)
    first = g_in is None
    whole = pl.BlockSpec((strip, width), lambda j: (0, 0))
    table = pl.BlockSpec((group, strip, side), lambda j: (j, 0, 0))
    in_specs = [
        pl.BlockSpec(memory_space=pltpu.SMEM),
        whole,
        pl.BlockSpec((width, strip), lambda j: (0, 0)),
        pl.BlockSpec((group, side, width), lambda j: (j, 0, 0)),
        table,
        table,
    ]
    operands = [tiles_in, users, users_t, panels, s_tab, n_tab]
    if not first:
        in_specs.append(whole)
        operands.append(g_in)
    return pl.pallas_call(
        functools.partial(grad_kernel, group, first),
        grid=(count // group,),
        out_shape=(
            jax.ShapeDtypeStruct((strip, width), jnp.float32),
            jax.ShapeDtypeStruct((count, width, side), out_dtype),
        ),
        in_specs=in_specs,
        out_specs=(whole, pl.BlockSpec((group, width, side), lambda j: (j, 0, 0))),
        compiler_params=pltpu.CompilerParams(vmem_limit_bytes=GRAD_VMEM),
        name="gradients",
    )(*operands)


def item_kernel(core, here, there, f_ref, a_ref, new_f, new_a):
    side = here.shape[1]
    mine = here[...].T
    theirs = there[...].T
    for k in range(2):
        rows = pl.ds(k * side, side)
        grad = jnp.where(core[0] == k, mine, theirs)
        total = a_ref[rows, :] + grad * grad
        new_a[rows, :] = total
        new_f[rows, :] = f_ref[rows, :] - grad / jnp.sqrt(total)


def update_items(core, here, there, factors, accum):
    vmem = pl.BlockSpec(memory_space=pltpu.VMEM)
    out = jax.ShapeDtypeStruct(factors.shape, jnp.float32)
    return pl.pallas_call(
        item_kernel,
        out_shape=(out, out),
        in_specs=[pl.BlockSpec(memory_space=pltpu.SMEM), vmem, vmem, vmem, vmem],
        out_specs=(vmem, vmem),
        compiler_params=pltpu.CompilerParams(vmem_limit_bytes=GRAD_VMEM),
        name="items",
    )(core.reshape(1), here, there, factors, accum)


def in_vmem(x):
    return pltpu.with_memory_space_constraint(x, pltpu.VMEM)


def in_hbm(x):
    return pltpu.with_memory_space_constraint(x, pltpu.HBM)


def local_dense(
    user_factors, user_accum, item_factors, item_accum, tile_counts, tile_user, tile_item, send_list
):
    side = tile_counts.shape[-1]
    tiles = tile_counts.shape[2]
    strip, _ = user_factors.shape
    blocks = strip // side
    peers = lax.axis_size("users")
    bits = peers.bit_length() - 1
    me = lax.axis_index("users")
    core = lax.axis_index("rep")
    axes = ("users", "rep")

    order_a = list(range(bits - 1, 1, -1)) + [0, 1]
    order_b = list(range(bits - 1, 1, -1))[::-1] + [1, 0]
    stages = list(zip(order_a, order_b))

    def swap(x, *chosen):
        masks = [sum(1 << stages[s][r] for s in chosen) for r in range(2)]
        pairs = [(2 * u + r, 2 * (u ^ masks[r]) + r) for u in range(peers) for r in range(2)]
        return lax.ppermute(x, axes, pairs)

    def other(x):
        return lax.ppermute(x, "rep", [(0, 1), (1, 0)])

    own_counts = tile_counts[0, 0]
    mine = lax.dynamic_slice_in_dim(item_factors, core * side, side, 0).astype(jnp.bfloat16)[None]
    got = swap(mine, 0) if bits > 2 else None
    code = tile_item[0, 0] * blocks + tile_user[0, 0]
    codes = jnp.concatenate([code, other(code)])
    par_counts = other(own_counts)
    counts = in_vmem(combine(in_hbm(own_counts), in_hbm(par_counts)))

    panel_id = codes // blocks
    distance = (panel_id // 2) ^ me
    position = jnp.zeros_like(distance)
    for s, (bit_a, bit_b) in enumerate(stages):
        bit = jnp.where(core == 0, bit_a, bit_b)
        position = position | (((distance >> bit) & 1) << s)
    pairs = peers * blocks
    keys = jnp.where(panel_id % 2 == core, position * blocks + codes % blocks, pairs)

    index = jnp.arange(2 * tiles, dtype=jnp.int32)
    before = (keys[None, :] < keys[:, None]) | (
        (keys[None, :] == keys[:, None]) & (index[None, :] < index[:, None])
    )
    rank = jnp.sum(before.astype(jnp.int32), axis=1)
    order = jnp.sum(jnp.where(rank[None, :] == index[:, None], index[None, :], 0), axis=1)
    pair = jnp.arange(pairs + blocks, dtype=jnp.int32)
    begin = jnp.sum((keys[None, :] < pair[:, None]).astype(jnp.int32), axis=1)
    weight = (begin[1 : pairs + 1] - begin[:pairs]).astype(jnp.float32) * ERR_SCALE

    span = peers // 4

    def tables(group):
        part = begin[group * span * blocks : ((group + 1) * span + 1) * blocks]
        return block_tables(order, part, counts, span, blocks)

    def block_grads(group, panels, table, g_in, out_dtype):
        weights = weight[group * span * blocks : (group + 1) * span * blocks]
        return gradients(weights, users, users_t, panels, *table, g_in, out_dtype)

    users, users_t = prepare_users(user_factors)
    panels = [mine]
    for s in range(bits - 2):
        if s:
            got = swap(panels[0], s)
        panels[0] = jnp.concatenate([panels[0], got], axis=0)
    panels.append(swap(panels[0], bits - 2))
    panels.append(swap(panels[0], bits - 1))
    panels.append(swap(panels[1], bits - 1))

    table = [tables(group) for group in range(4)]

    grad, send = block_grads(2, panels[2], table[2], None, jnp.bfloat16)
    got_0 = swap(send, bits - 1)
    grad, send = block_grads(3, panels[3], table[3], grad, jnp.bfloat16)
    got_1 = swap(send, bits - 1)
    grad, keep_1 = block_grads(1, panels[1], table[1], grad, jnp.float32)
    grad, keep_0 = block_grads(0, panels[0], table[0], grad, jnp.float32)

    send = (keep_1 + got_1.astype(jnp.float32)).astype(jnp.bfloat16)
    held = keep_0 + got_0.astype(jnp.float32)
    held = held + swap(send, bits - 2).astype(jnp.float32)
    grad_there = other(grad)
    for s in range(bits - 3, 1, -1):
        span = span // 2
        held = held[:span] + swap(held[span:], s)
    parts = []
    for d in range(span - 1, 0, -1):
        chosen = [s for s in range(2) if d >> s & 1]
        parts.append(swap(held[d].astype(jnp.bfloat16), *chosen))
    here = held[0]
    for part in parts:
        here = here + part.astype(jnp.float32)

    new_users, new_user_accum = adagrad(user_factors, user_accum, grad + grad_there)

    there = other(here)
    new_items, new_item_accum = update_items(core, here, there, item_factors, item_accum)
    return (new_users, new_user_accum, new_items, new_item_accum)


def solution(mesh):
    peers = mesh.shape["users"]


    def local(*args):
        side = args[4].shape[-1]
        table_bytes = peers * args[0].shape[0] * side * 2 * 2
        dense = (
            mesh.shape["rep"] == 2
            and args[2].shape[0] == 2 * side
            and peers >= 4
            and peers & (peers - 1) == 0
            and table_bytes <= DENSE_LIMIT
        )
        return (local_dense if dense else local_tiles)(*args)

    return jax.shard_map(
        local,
        mesh=mesh,
        in_specs=(
            P("users", None),
            P("users", None),
            P("users", None),
            P("users", None),
            P("users", "rep", None, None, None),
            P("users", "rep", None),
            P("users", "rep", None),
            P("users", "rep", None),
        ),
        out_specs=(P("users", None), P("users", None), P("users", None), P("users", None)),
        check_vma=False,
    )
```

```python
import functools
import math

import jax
import jax.numpy as jnp
from jax import lax
from jax.experimental import pallas as pl
from jax.experimental.pallas import tpu as pltpu
from jax.sharding import PartitionSpec as P


CONF_SLOPE = 0.5
ERR_SCALE = 1.0 / 64.0
DENSE_LIMIT = 32 * 1024 * 1024
TABLE_VMEM = 24 * 1024 * 1024
GRAD_VMEM = 32 * 1024 * 1024
TWO_PART = True
GROUP = 4


def tile_terms(user_strip, panels, counts, users_idx, fetch_index, slot_index, slot_count):
    tile_count = counts.shape[0]
    group_size = math.gcd(tile_count, 32)
    group_count = tile_count // group_size
    side = counts.shape[-1]
    width = panels.shape[-1]

    def tile_step(totals, inputs):
        user_total, slot_total = totals
        block_counts, block_user, block_fetch, block_slot = inputs
        user_rows = user_strip[block_user]
        item_rows = panels[block_fetch]
        predicted = jnp.einsum(
            "gur,gir->gui", user_rows, item_rows, preferred_element_type=jnp.float32
        )
        amount = block_counts.astype(jnp.float32)
        confidence = 1.0 + CONF_SLOPE * amount
        preference = jnp.where(amount > 0, 1.0, 0.0).astype(jnp.float32)
        weighted_err = (confidence * (predicted - preference) * ERR_SCALE).astype(jnp.bfloat16)
        user_part = jnp.einsum(
            "gui,gir->gur", weighted_err, item_rows, preferred_element_type=jnp.float32
        )
        item_part = jnp.einsum(
            "gui,gur->gir", weighted_err, user_rows, preferred_element_type=jnp.float32
        )
        user_total = user_total.at[block_user].add(user_part)
        slot_total = slot_total.at[block_slot].add(item_part)
        return ((user_total, slot_total), None)

    start = (
        jnp.zeros((user_strip.shape[0], side, width), jnp.float32),
        jnp.zeros((slot_count, side, width), jnp.float32),
    )
    inputs = (
        counts.reshape(group_count, group_size, side, side),
        users_idx.reshape(group_count, group_size),
        fetch_index.reshape(group_count, group_size),
        slot_index.reshape(group_count, group_size),
    )
    (user_total, slot_total), _ = lax.scan(tile_step, start, inputs)
    return (user_total, slot_total)


def adagrad(factors, accum, grad):
    new_accum = accum + grad * grad
    return (factors - grad / jnp.sqrt(new_accum), new_accum)


def local_tiles(
    user_factors, user_accum, item_factors, item_accum, tile_counts, tile_user, tile_item, send_list
):
    tile_size = tile_counts.shape[-1]
    feat_width = user_factors.shape[1]
    user_strip = user_factors.astype(jnp.bfloat16).reshape(-1, tile_size, feat_width)
    owned_panels = item_factors.astype(jnp.bfloat16).reshape(-1, tile_size, feat_width)
    panels_own = owned_panels.shape[0]
    peer_count = lax.axis_size("users")
    counts = tile_counts[0, 0]
    users_idx = tile_user[0, 0]
    items_idx = tile_item[0, 0]
    send_row = send_list[0, 0]
    slot_index = items_idx // panels_own
    outgoing = owned_panels[jnp.minimum(send_row, panels_own - 1)]
    panels = lax.all_to_all(outgoing, "users", split_axis=0, concat_axis=0, tiled=True)
    user_part, slot_part = tile_terms(
        user_strip, panels, counts, users_idx, slot_index, slot_index, peer_count
    )
    returned = lax.all_to_all(
        slot_part.astype(jnp.bfloat16), "users", split_axis=0, concat_axis=0, tiled=True
    )
    selector = (send_row[None, :] == jnp.arange(panels_own, dtype=jnp.int32)[:, None]).astype(
        jnp.bfloat16
    )
    item_part = jnp.einsum("kq,qir->kir", selector, returned, preferred_element_type=jnp.float32)
    item_part = item_part.reshape(-1, feat_width)
    user_grad = lax.psum(user_part.reshape(-1, feat_width), "rep")
    new_users, new_user_accum = adagrad(user_factors, user_accum, user_grad)
    item_grad = lax.psum(item_part, "rep")
    new_items, new_item_accum = adagrad(item_factors, item_accum, item_grad)
    return (new_users, new_user_accum, new_items, new_item_accum)


def combine_kernel(own, par, out, zeros, sems):
    tiles = own.shape[0]
    zeros[...] = jnp.zeros_like(zeros)
    copies = [
        pltpu.make_async_copy(own, out.at[pl.ds(0, tiles)], sems.at[0]),
        pltpu.make_async_copy(par, out.at[pl.ds(tiles, tiles)], sems.at[1]),
        pltpu.make_async_copy(zeros, out.at[pl.ds(2 * tiles, 1)], sems.at[2]),
    ]
    for copy in copies:
        copy.start()
    for copy in copies:
        copy.wait()


def combine(own, par):
    tiles, side, _ = own.shape
    anywhere = pl.BlockSpec(memory_space=pl.ANY)
    return pl.pallas_call(
        combine_kernel,
        out_shape=jax.ShapeDtypeStruct((2 * tiles + 1, side, side), own.dtype),
        in_specs=[anywhere, anywhere],
        out_specs=anywhere,
        scratch_shapes=[
            pltpu.VMEM((1, side, side), own.dtype),
            pltpu.SemaphoreType.DMA((3,)),
        ],
        compiler_params=pltpu.CompilerParams(vmem_limit_bytes=TABLE_VMEM),
        name="combine",
    )(own, par)


def table_kernel(order, begin, counts, s_ref, n_ref):
    positions, strip, side = s_ref.shape
    blocks = strip // side
    last = order.shape[0] - 1
    empty = counts.shape[0] - 1

    def terms(tile):
        count = counts[tile]
        hit = jnp.where(count > 0, jnp.bfloat16(ERR_SCALE), jnp.bfloat16(0.0))
        return count.astype(jnp.float32) * (CONF_SLOPE * ERR_SCALE), hit

    def position(step, _):
        for ub in range(blocks):
            pair = step * blocks + ub
            rows = slice(ub * side, (ub + 1) * side)
            first = begin[pair]
            used = first < begin[pair + 1]
            half, hit = terms(jnp.where(used, order[jnp.minimum(first, last)], empty))
            s_ref[step, rows, :] = half
            n_ref[step, rows, :] = hit

        def block(ub, _):
            pair = step * blocks + ub
            rows = pl.ds(pl.multiple_of(ub * side, side), side)

            def more(k, _):
                half, hit = terms(order[k])
                s_ref[step, rows, :] += half
                n_ref[step, rows, :] += hit
                return 0

            lax.fori_loop(begin[pair] + 1, begin[pair + 1], more, 0)
            return 0

        lax.fori_loop(0, blocks, block, 0)
        return 0

    lax.fori_loop(0, positions, position, 0)


def block_tables(order, begin, counts, positions, blocks):
    side = counts.shape[-1]
    shape = (positions, blocks * side, side)
    scalars = pl.BlockSpec(memory_space=pltpu.SMEM)
    whole = pl.BlockSpec(memory_space=pltpu.VMEM)
    return pl.pallas_call(
        table_kernel,
        out_shape=(
            jax.ShapeDtypeStruct(shape, jnp.float32),
            jax.ShapeDtypeStruct(shape, jnp.bfloat16),
        ),
        in_specs=[scalars, scalars, whole],
        out_specs=(whole, whole),
        compiler_params=pltpu.CompilerParams(vmem_limit_bytes=TABLE_VMEM),
        name="tables",
    )(order, begin, counts)


def prepare_kernel(f_ref, u_ref, ut_ref):
    rounded = f_ref[...].astype(jnp.bfloat16)
    u_ref[...] = rounded
    ut_ref[...] = f_ref[...].T.astype(jnp.bfloat16)


def prepare_users(factors):
    strip, width = factors.shape
    step = math.gcd(strip, 512)
    return pl.pallas_call(
        prepare_kernel,
        grid=(strip // step,),
        out_shape=(
            jax.ShapeDtypeStruct((strip, width), jnp.bfloat16),
            jax.ShapeDtypeStruct((width, strip), jnp.bfloat16),
        ),
        in_specs=[pl.BlockSpec((step, width), lambda j: (j, 0))],
        out_specs=(
            pl.BlockSpec((step, width), lambda j: (j, 0)),
            pl.BlockSpec((width, step), lambda j: (0, j)),
        ),
        compiler_params=pltpu.CompilerParams(vmem_limit_bytes=GRAD_VMEM),
        name="prepare",
    )(factors)


def grad_kernel(group, first, tiles_in, u_ref, ut_ref, v_ref, s_ref, n_ref, *refs):
    if first:
        g_ref, p_ref = refs
    else:
        gin_ref, g_ref, p_ref = refs
    step = pl.program_id(0)
    side = s_ref.shape[-1]
    users = u_ref.shape[0]
    blocks = users // side

    @pl.when(step == 0)
    def _():
        g_ref[...] = jnp.zeros_like(g_ref) if first else gin_ref[...]

    panel = v_ref[...].reshape(group * side, v_ref.shape[-1])
    predicted = lax.dot_general(
        u_ref[...], panel, (((1,), (1,)), ((), ())), preferred_element_type=jnp.float32
    )

    columns, rests = [], []
    for k in range(group):
        rows, low = [], []
        for ub in range(blocks):
            weight = tiles_in[(step * group + k) * blocks + ub]
            part = slice(ub * side, (ub + 1) * side)
            half = s_ref[k, part, :]
            hits = n_ref[k, part, :].astype(jnp.float32)
            guess = predicted[part, k * side : (k + 1) * side]
            err = (weight + half) * guess - (hits + half)
            rows.append(err.astype(jnp.bfloat16))
            if TWO_PART:
                low.append((err - rows[-1].astype(jnp.float32)).astype(jnp.bfloat16))
        columns.append(jnp.concatenate(rows, axis=0))
        if TWO_PART:
            rests.append(jnp.concatenate(low, axis=0))
    err = jnp.concatenate(columns, axis=1)
    total = jnp.dot(err, panel, preferred_element_type=jnp.float32)
    item = jnp.dot(ut_ref[...], err, preferred_element_type=jnp.float32)
    if TWO_PART:
        rest = jnp.concatenate(rests, axis=1)
        total += jnp.dot(rest, panel, preferred_element_type=jnp.float32)
        item += jnp.dot(ut_ref[...], rest, preferred_element_type=jnp.float32)
    g_ref[...] += total
    for k in range(group):
        p_ref[k] = item[:, k * side : (k + 1) * side].astype(p_ref.dtype)


def gradients(tiles_in, users, users_t, panels, s_tab, n_tab, g_in, out_dtype):
    count, side, width = panels.shape
    strip = users.shape[0]
    group = math.gcd(count, GROUP)
    first = g_in is None
    whole = pl.BlockSpec((strip, width), lambda j: (0, 0))
    table = pl.BlockSpec((group, strip, side), lambda j: (j, 0, 0))
    in_specs = [
        pl.BlockSpec(memory_space=pltpu.SMEM),
        whole,
        pl.BlockSpec((width, strip), lambda j: (0, 0)),
        pl.BlockSpec((group, side, width), lambda j: (j, 0, 0)),
        table,
        table,
    ]
    operands = [tiles_in, users, users_t, panels, s_tab, n_tab]
    if not first:
        in_specs.append(whole)
        operands.append(g_in)
    return pl.pallas_call(
        functools.partial(grad_kernel, group, first),
        grid=(count // group,),
        out_shape=(
            jax.ShapeDtypeStruct((strip, width), jnp.float32),
            jax.ShapeDtypeStruct((count, width, side), out_dtype),
        ),
        in_specs=in_specs,
        out_specs=(whole, pl.BlockSpec((group, width, side), lambda j: (j, 0, 0))),
        compiler_params=pltpu.CompilerParams(vmem_limit_bytes=GRAD_VMEM),
        name="gradients",
    )(*operands)


def item_kernel(core, here, there, f_ref, a_ref, new_f, new_a):
    side = here.shape[1]
    mine = here[...].T
    theirs = there[...].T
    for k in range(2):
        rows = pl.ds(k * side, side)
        grad = jnp.where(core[0] == k, mine, theirs)
        total = a_ref[rows, :] + grad * grad
        new_a[rows, :] = total
        new_f[rows, :] = f_ref[rows, :] - grad / jnp.sqrt(total)


def update_items(core, here, there, factors, accum):
    vmem = pl.BlockSpec(memory_space=pltpu.VMEM)
    out = jax.ShapeDtypeStruct(factors.shape, jnp.float32)
    return pl.pallas_call(
        item_kernel,
        out_shape=(out, out),
        in_specs=[pl.BlockSpec(memory_space=pltpu.SMEM), vmem, vmem, vmem, vmem],
        out_specs=(vmem, vmem),
        compiler_params=pltpu.CompilerParams(vmem_limit_bytes=GRAD_VMEM),
        name="items",
    )(core.reshape(1), here, there, factors, accum)


def in_vmem(x):
    return pltpu.with_memory_space_constraint(x, pltpu.VMEM)


def in_hbm(x):
    return pltpu.with_memory_space_constraint(x, pltpu.HBM)


def local_dense(
    user_factors, user_accum, item_factors, item_accum, tile_counts, tile_user, tile_item, send_list
):
    side = tile_counts.shape[-1]
    tiles = tile_counts.shape[2]
    strip, _ = user_factors.shape
    blocks = strip // side
    peers = lax.axis_size("users")
    bits = peers.bit_length() - 1
    me = lax.axis_index("users")
    core = lax.axis_index("rep")
    axes = ("users", "rep")

    order_a = list(range(bits - 1, 1, -1)) + [0, 1]
    order_b = list(range(bits - 1, 1, -1))[::-1] + [1, 0]
    stages = list(zip(order_a, order_b))

    def swap(x, *chosen):
        masks = [sum(1 << stages[s][r] for s in chosen) for r in range(2)]
        pairs = [(2 * u + r, 2 * (u ^ masks[r]) + r) for u in range(peers) for r in range(2)]
        return lax.ppermute(x, axes, pairs)

    def other(x):
        return lax.ppermute(x, "rep", [(0, 1), (1, 0)])

    own_counts = tile_counts[0, 0]
    mine = lax.dynamic_slice_in_dim(item_factors, core * side, side, 0).astype(jnp.bfloat16)[None]
    got = swap(mine, 0) if bits > 2 else None
    code = tile_item[0, 0] * blocks + tile_user[0, 0]
    codes = jnp.concatenate([code, other(code)])
    par_counts = other(own_counts)
    counts = in_vmem(combine(in_hbm(own_counts), in_hbm(par_counts)))

    panel_id = codes // blocks
    distance = (panel_id // 2) ^ me
    position = jnp.zeros_like(distance)
    for s, (bit_a, bit_b) in enumerate(stages):
        bit = jnp.where(core == 0, bit_a, bit_b)
        position = position | (((distance >> bit) & 1) << s)
    pairs = peers * blocks
    keys = jnp.where(panel_id % 2 == core, position * blocks + codes % blocks, pairs)

    index = jnp.arange(2 * tiles, dtype=jnp.int32)
    before = (keys[None, :] < keys[:, None]) | (
        (keys[None, :] == keys[:, None]) & (index[None, :] < index[:, None])
    )
    rank = jnp.sum(before.astype(jnp.int32), axis=1)
    order = jnp.sum(jnp.where(rank[None, :] == index[:, None], index[None, :], 0), axis=1)
    pair = jnp.arange(pairs + blocks, dtype=jnp.int32)
    begin = jnp.sum((keys[None, :] < pair[:, None]).astype(jnp.int32), axis=1)
    weight = (begin[1 : pairs + 1] - begin[:pairs]).astype(jnp.float32) * ERR_SCALE

    span = peers // 4

    def tables(group):
        part = begin[group * span * blocks : ((group + 1) * span + 1) * blocks]
        return block_tables(order, part, counts, span, blocks)

    def block_grads(group, panels, table, g_in, out_dtype):
        weights = weight[group * span * blocks : (group + 1) * span * blocks]
        return gradients(weights, users, users_t, panels, *table, g_in, out_dtype)

    users, users_t = prepare_users(user_factors)
    panels = [mine]
    for s in range(bits - 2):
        if s:
            got = swap(panels[0], s)
        panels[0] = jnp.concatenate([panels[0], got], axis=0)
    panels.append(swap(panels[0], bits - 2))
    panels.append(swap(panels[0], bits - 1))
    panels.append(swap(panels[1], bits - 1))

    table = [tables(group) for group in range(4)]

    grad, send = block_grads(2, panels[2], table[2], None, jnp.bfloat16)
    got_0 = swap(send, bits - 1)
    grad, send = block_grads(3, panels[3], table[3], grad, jnp.bfloat16)
    got_1 = swap(send, bits - 1)
    grad, keep_1 = block_grads(1, panels[1], table[1], grad, jnp.float32)
    grad, keep_0 = block_grads(0, panels[0], table[0], grad, jnp.float32)

    send = (keep_1 + got_1.astype(jnp.float32)).astype(jnp.bfloat16)
    held = keep_0 + got_0.astype(jnp.float32)
    held = held + swap(send, bits - 2).astype(jnp.float32)
    grad_there = other(grad)
    for s in range(bits - 3, 1, -1):
        span = span // 2
        held = held[:span] + swap(held[span:], s)
    parts = []
    for d in range(span - 1, 0, -1):
        chosen = [s for s in range(2) if d >> s & 1]
        parts.append(swap(held[d].astype(jnp.bfloat16), *chosen))
    here = held[0]
    for part in parts:
        here = here + part.astype(jnp.float32)

    new_users, new_user_accum = adagrad(user_factors, user_accum, grad + grad_there)

    there = other(here)
    new_items, new_item_accum = update_items(core, here, there, item_factors, item_accum)
    return (new_users, new_user_accum, new_items, new_item_accum)


def solution(mesh):
    peers = mesh.shape["users"]


    def local(*args):
        side = args[4].shape[-1]
        table_bytes = peers * args[0].shape[0] * side * 2 * 2
        dense = (
            mesh.shape["rep"] == 2
            and args[2].shape[0] == 2 * side
            and peers >= 4
            and peers & (peers - 1) == 0
            and table_bytes <= DENSE_LIMIT
        )
        return (local_dense if dense else local_tiles)(*args)

    return jax.shard_map(
        local,
        mesh=mesh,
        in_specs=(
            P("users", None),
            P("users", None),
            P("users", None),
            P("users", None),
            P("users", "rep", None, None, None),
            P("users", "rep", None),
            P("users", "rep", None),
            P("users", "rep", None),
        ),
        out_specs=(P("users", None), P("users", None), P("users", None), P("users", None)),
        check_vma=False,
    )
```
